32 devices in a mesh: dp: 4 (over y, x), tm: 4 (over z), height: 2 (over core).
Axes of the slice: x: 2, y: 2, z: 4, core: 2. Of those that a mesh axis runs over, the one named last changes fastest.
Arguments:
- latents: bfloat16 [4, 8, 8, 160, 128], P('dp', 'tm', 'height'), may hold values from -40 to 40
- cotangent: bfloat16 [4, 8, 16, 320, 128], P('dp', 'tm', 'height'), may hold values from -6 to 6
- group_norm_gain: float32 [128], replicated, may hold values from 0.5 to 1.5
- group_norm_bias: float32 [128], replicated, may hold values from -3 to 3
- kernel: bfloat16 [3, 3, 384, 128], replicated, may hold values from -0.109375 to 0.109375
- kernel_bias: float32 [128], replicated, may hold values from -3 to 3
Outputs:
- upsampled: bfloat16 [4, 8, 16, 320, 128], P('dp', 'tm', 'height')
- latent_gradient: bfloat16 [4, 8, 8, 160, 128], P('dp', 'tm', 'height')
- kernel_grad: float32 [3, 3, 384, 128], replicated
- bias_grad: float32 [128], replicated
- gain_grad: float32 [128], replicated
- shift_grad: float32 [128], replicated
The draws below stay inside these ranges and needn't reach their ends.
All inputs are finite; a program needn't handle non-finite values.
Results may differ from the reference program's by a relative error of at most 0.0051.
Values may be sent and summed in bfloat16 or wider, within the bound.
No kernel may reach another device: no remote copies, remote signals or barrier semaphores. Data moves between devices by JAX's collectives and lax.ppermute only.
A program may use at most 128 MiB of HBM per device.

```python
import jax
import jax.numpy as jnp
from jax import lax

C = 128
GROUPS = 32
WIDTH = 160
CLIPS = 4
FRAMES = 8
ROWS = 8


def draw_latents(key, part):
    shape = (CLIPS, FRAMES, ROWS, WIDTH, C)
    key_noise, key_rough, key_offset = jax.random.split(key, 3)
    frame_pos = jnp.arange(FRAMES, dtype=jnp.float32) / max(FRAMES - 1, 1)
    row_pos = jnp.arange(ROWS, dtype=jnp.float32) / max(ROWS - 1, 1)
    rising = 3.0 ** (0.5 * (frame_pos[:, None] + row_pos[None, :]))
    rough = jnp.exp(jax.random.uniform(key_rough, (CLIPS, FRAMES, ROWS, WIDTH, 1), jnp.float32, -0.7, 0.7))
    noise = jax.random.normal(key_noise, shape, jnp.float32)
    offset = jax.random.normal(key_offset, (CLIPS, 1, 1, 1, C), jnp.float32) * 0.5
    value = noise * rough * rising[None, :, :, None, None] + offset
    return jnp.clip(value, -40.0, 40.0).astype(jnp.bfloat16)


def level_of(own_key, shape, cuts, low, top_value):
    def one(axis_at, blocks):
        draws = jax.random.uniform(jax.random.fold_in(jax.random.fold_in(own_key, 6), axis_at), (blocks,), jnp.float32, low / len(cuts), top_value / len(cuts))
        return jnp.repeat(jnp.exp(draws), shape[axis_at] // blocks).reshape((-1,) + (1,) * (len(shape) - axis_at - 1))

    gain = one(*cuts[0])
    for cut in cuts[1:]:
        gain = gain * one(*cut)
    return gain


def normal_values(own_key, shape, deviation, most, pieces=(), kind=jnp.bfloat16):
    level = level_of(own_key, shape, pieces, -0.22, 0.18) if pieces else 1.0
    entries = jax.random.normal(own_key, shape, jnp.float32) * deviation * level
    return jnp.minimum(jnp.maximum(entries, -most), most).astype(kind)


def setup_inputs(seed: int = 0) -> dict:
    streams_of = jax.random.split(jax.random.key(seed), 7)
    latents = draw_latents(jax.random.fold_in(streams_of[6], 71), 0)
    cotangent = normal_values(streams_of[1], (CLIPS, FRAMES, 2 * ROWS, 2 * WIDTH, C), 1.0, 6.0, ((0, 4), (1, 4), (2, 2)))
    group_norm_gain = jnp.clip(jax.random.uniform(streams_of[2], (C,), jnp.float32, 0.5, 1.5), 0.5, 1.5)
    group_norm_bias = normal_values(streams_of[3], (C,), 0.5, 3.0, (), jnp.float32)
    kernel = normal_values(streams_of[4], (3, 3, 3 * C, C), (27 * C) ** -0.5, 0.109375)
    kernel_bias = normal_values(streams_of[5], (C,), 0.5, 3.0, (), jnp.float32)
    return dict(latents=latents, cotangent=cotangent, group_norm_gain=group_norm_gain, group_norm_bias=group_norm_bias, kernel=kernel, kernel_bias=kernel_bias)


def conv(padded, kernel, out_t, out_r, out_w):
    total = jnp.zeros((out_t * out_r * out_w, kernel.shape[-1]), jnp.float32)
    for i in range(3):
        for j in range(3):
            slab = jnp.concatenate([padded[i:i + out_t, j:j + out_r, k:k + out_w] for k in range(3)], axis=-1)
            total = total + jnp.dot(slab.reshape(-1, slab.shape[-1]), kernel[i, j], preferred_element_type=jnp.float32)
    return total.reshape(out_t, out_r, out_w, kernel.shape[-1])

def kernel_terms(padded, grad_out):
    out_t, out_r, out_w, channel_total = grad_out.shape
    flat = grad_out.reshape(-1, channel_total)
    rows_all = []
    for i in range(3):
        row_list = []
        for j in range(3):
            slab = jnp.concatenate([padded[i:i + out_t, j:j + out_r, k:k + out_w] for k in range(3)], axis=-1)
            row_list.append(lax.dot_general(slab.reshape(-1, slab.shape[-1]), flat, (((0,), (0,)), ((), ())), preferred_element_type=jnp.float32))
        rows_all.append(jnp.stack(row_list))
    return jnp.stack(rows_all)

def flip_kernel(kernel):
    channel_total = kernel.shape[-1]
    split = kernel.reshape(3, 3, 3, channel_total, channel_total)[::-1, ::-1, ::-1]
    return jnp.swapaxes(split, 3, 4).reshape(3, 3, 3 * channel_total, channel_total)

def edge_pad(value):
    return jnp.pad(value, ((2, 0), (1, 1), (1, 1), (0, 0)), mode='edge')

def one_clip(latent, cot, group_norm_gain, group_norm_bias, kernel, kernel_bias):
    frame_total, row_total, width_total, channel_total = latent.shape
    group_size = channel_total // GROUPS
    grouped = latent.astype(jnp.float32).reshape(frame_total, row_total, width_total, GROUPS, group_size)
    group_mean = lax.optimization_barrier(jnp.mean(grouped, axis=(0, 1, 2, 4)))
    centred_input = grouped - group_mean[:, None]
    var = lax.optimization_barrier(jnp.mean(centred_input * centred_input, axis=(0, 1, 2, 4)))
    inverse_deviation = lax.rsqrt(var + 1e-06)
    normalized_times_gradient = centred_input * inverse_deviation[:, None]
    normalized_input = normalized_times_gradient.reshape(frame_total, row_total, width_total, channel_total)
    preactivation = normalized_input * group_norm_gain + group_norm_bias
    sig = jax.nn.sigmoid(preactivation)
    act = (preactivation * sig).astype(jnp.bfloat16)
    padded = edge_pad(act)
    conv_out = (conv(padded, kernel, frame_total, row_total, width_total) + kernel_bias).astype(jnp.bfloat16)
    upsampled = jnp.broadcast_to(conv_out[:, :, None, :, None, :], (frame_total, row_total, 2, width_total, 2, channel_total)).reshape(frame_total, 2 * row_total, 2 * width_total, channel_total)
    dconv32 = lax.optimization_barrier(jnp.sum(cot.astype(jnp.float32).reshape(frame_total, row_total, 2, width_total, 2, channel_total), axis=(2, 4)))
    bias_part = lax.optimization_barrier(jnp.sum(dconv32, axis=(0, 1, 2)))
    dconv = dconv32.astype(jnp.bfloat16)
    kernel_part = kernel_terms(padded, dconv)
    wide = jnp.pad(dconv, ((2, 2), (2, 2), (2, 2), (0, 0)))
    dpadded = conv(wide, flip_kernel(kernel), frame_total + 2, row_total + 2, width_total + 2)
    primal, pull = jax.vjp(edge_pad, jnp.zeros((frame_total, row_total, width_total, channel_total), jnp.float32))
    dact = pull(dpadded)[0]
    preact_gradient = dact * sig * (1.0 + preactivation * (1.0 - sig))
    gain_partial = lax.optimization_barrier(jnp.sum(preact_gradient * normalized_input, axis=(0, 1, 2)))
    shift_part = lax.optimization_barrier(jnp.sum(preact_gradient, axis=(0, 1, 2)))
    normalized_gradient = (preact_gradient * group_norm_gain).reshape(frame_total, row_total, width_total, GROUPS, group_size)
    first_mean = lax.optimization_barrier(jnp.mean(normalized_gradient, axis=(0, 1, 2, 4)))
    second_mean = lax.optimization_barrier(jnp.mean(normalized_gradient * normalized_times_gradient, axis=(0, 1, 2, 4)))
    latent_gradient = (inverse_deviation[:, None] * (normalized_gradient - first_mean[:, None] - normalized_times_gradient * second_mean[:, None])).reshape(frame_total, row_total, width_total, channel_total).astype(jnp.bfloat16)
    return (upsampled, latent_gradient, kernel_part, bias_part, gain_partial, shift_part)

def reference(latents, cotangent, group_norm_gain, group_norm_bias, kernel, kernel_bias):

    def step(pair):
        return one_clip(pair[0], pair[1], group_norm_gain, group_norm_bias, kernel, kernel_bias)
    upsampled, latent_gradient, kernel_parts, bias_parts, gain_parts, shift_parts = lax.map(step, (latents, cotangent))
    return (upsampled, latent_gradient, lax.optimization_barrier(jnp.sum(kernel_parts, axis=0)), lax.optimization_barrier(jnp.sum(bias_parts, axis=0)), lax.optimization_barrier(jnp.sum(gain_parts, axis=0)), lax.optimization_barrier(jnp.sum(shift_parts, axis=0)))
```

```python
import functools

import jax
import jax.numpy as jnp
from jax import lax
from jax.experimental import pallas as pl
from jax.experimental.pallas import tpu as pltpu
from jax.sharding import PartitionSpec as P

GROUPS = 32
F32 = jnp.float32
BF16 = jnp.bfloat16
TAB = 32
VMEM = pl.BlockSpec(memory_space=pltpu.VMEM)


def call(body, outs, *args, scratch=(), flops=1_000_000):
    moved = sum(a.size * a.dtype.itemsize for a in (*args, *outs))
    return pl.pallas_call(
        body,
        out_shape=tuple(outs),
        in_specs=[VMEM] * len(args),
        out_specs=tuple([VMEM] * len(outs)),
        scratch_shapes=list(scratch),
        cost_estimate=pl.CostEstimate(flops=flops, bytes_accessed=moved, transcendentals=0),
    )(*args)


def shape(dims, dtype):
    return jax.ShapeDtypeStruct(dims, dtype)


def swap(block, axis, distance):
    count = lax.axis_size(axis)
    return lax.ppermute(block, axis, [(i, i ^ distance) for i in range(count)])


def moved(block, frames, rows):
    n_t, n_h = lax.axis_size("tm"), lax.axis_size("height")
    route = []
    for t in range(n_t):
        for h in range(n_h):
            if 0 <= t + frames < n_t and 0 <= h + rows < n_h:
                route.append(((t + frames) * n_h + h + rows, t * n_h + h))
    return lax.ppermute(block, ("tm", "height"), route)


def across(block, frames):
    n_t = lax.axis_size("tm")
    route = []
    for t in range(n_t):
        for h in range(2):
            if 0 <= t + frames < n_t:
                route.append(((t + frames) * 2 + 1 - h, t * 2 + h))
    return lax.ppermute(block, ("tm", "height"), route)


def facing(edges, frames):
    if len(edges) == 1:
        other = across(edges[0], frames)
        return [other]
    return [moved(edges[0], frames, -1), moved(edges[1], frames, 1)]


def tree(values):
    while len(values) > 1:
        values = [values[i] + values[i + 1] for i in range(0, len(values), 2)]
    return values[0]


def group_sum(x):
    lane = lax.broadcasted_iota(jnp.int32, x.shape, 1)
    n = x.shape[1]
    x = x + jnp.where(lane % 2 == 0, pltpu.roll(x, n - 1, 1), pltpu.roll(x, 1, 1))
    return x + jnp.where(lane % 4 < 2, pltpu.roll(x, n - 2, 1), pltpu.roll(x, 2, 1))


def packed(table):
    high = table.astype(BF16).astype(F32)
    rest = table - high
    mid = rest.astype(BF16).astype(F32)
    low = (rest - mid).astype(BF16).astype(F32)
    return jnp.concatenate([high, mid, low, jnp.zeros_like(low)], axis=0).astype(BF16)


def unpacked(rows):
    rows = rows.astype(F32)
    return (rows[0:8] + rows[8:16]) + rows[16:24]


def before(x, edge):
    row = lax.broadcasted_iota(jnp.int32, x.shape, 0)
    return jnp.where(row == 0, x if edge else 0.0, pltpu.roll(x, 1, 0))


def after(x, edge):
    row = lax.broadcasted_iota(jnp.int32, x.shape, 0)
    return jnp.where(row == x.shape[0] - 1, x if edge else 0.0, pltpu.roll(x, x.shape[0] - 1, 0))


def stats_body(lat_ref, out_ref):
    t_n, r_n, w_n, c_n = lat_ref.shape
    total = jnp.zeros((8, c_n), F32)
    for t in range(t_n):
        for r in range(r_n):
            total += jnp.sum(lat_ref[t, r].astype(F32).reshape(w_n // 8, 8, c_n), axis=0)
    mean = jnp.sum(total, axis=0, keepdims=True) / (t_n * r_n * w_n)
    square = jnp.zeros((8, c_n), F32)
    for t in range(t_n):
        for r in range(r_n):
            x = (lat_ref[t, r].astype(F32) - mean).reshape(w_n // 8, 8, c_n)
            square += jnp.sum(x * x, axis=0)
    square = jnp.sum(square, axis=0, keepdims=True)
    row = lax.broadcasted_iota(jnp.int32, (8, c_n), 0)
    out_ref[...] = jnp.where(row == 0, mean, jnp.where(row == 1, square, 0.0))


def fold_body(edge_n, cot_ref, out_ref, bias_ref, *rest):
    edge_refs, wide = rest[:edge_n], rest[edge_n]
    t_n, r2, w2, c_n = cot_ref.shape
    r_n, w_n = r2 // 2, w2 // 2
    total = jnp.zeros((8, c_n), F32)
    for t in range(t_n):
        for r in range(r_n):
            slot = (t * r_n + r) % 2
            wide[slot] = cot_ref[t, 2 * r].astype(F32) + cot_ref[t, 2 * r + 1].astype(F32)
            value = wide[slot, pl.ds(0, w_n, stride=2), :] + wide[slot, pl.ds(1, w_n, stride=2), :]
            total += jnp.sum(value.reshape(w_n // 8, 8, c_n), axis=0)
            out_ref[t, r] = value.astype(BF16)
    bias_ref[...] = jnp.broadcast_to(jnp.sum(total, axis=0, keepdims=True), (8, c_n))
    edges(out_ref, edge_refs, r_n)


def edges(ref, edge_refs, r_n):
    if len(edge_refs) == 1:
        row = jnp.where(lax.axis_index("height") == 0, r_n - 1, 0)
        edge_refs[0][...] = ref[:, row]
    else:
        edge_refs[0][...] = ref[:, r_n - 1]
        edge_refs[1][...] = ref[:, 0]


def main_body(
    n_edge, cells, n_h,
    lat_ref, mine_ref, other_ref, grad_ref, halo_ref, kernel_ref, gain_ref, shift_ref, bias_ref, *rest,
):
    edge_refs, corner_refs, rest = rest[:n_edge], rest[n_edge : 2 * n_edge], rest[2 * n_edge :]
    keep_ref, table_ref, dpre_ref, norm_ref = rest[:4]
    send_refs, (acts, fold, weight, slope, hats, sums) = rest[4 : 3 + n_h], rest[3 + n_h :]
    t_n, r_n, w_n, c_n = lat_ref.shape
    h = lax.axis_index("height")
    top = (h == 0).astype(F32)
    bottom = (h == n_h - 1).astype(F32)
    first = (lax.axis_index("tm") == 0).astype(F32)

    a, b = mine_ref[...], other_ref[...]
    gap = a[0:1] - b[0:1]
    channel_mean = (a[0:1] + b[0:1]) * 0.5
    square = a[1:2] + b[1:2] + gap * gap * (cells / 4)
    channel_mean = jnp.broadcast_to(channel_mean, (8, c_n))
    size = c_n // GROUPS
    mean = group_sum(channel_mean) * (1.0 / size)
    off = channel_mean - mean
    var = group_sum(jnp.broadcast_to(square, (8, c_n)) + off * off * cells) * (1.0 / (cells * size))
    rstd = lax.rsqrt(var + 1e-06)
    row = lax.broadcasted_iota(jnp.int32, (8, c_n), 0)
    norm_ref[...] = jnp.where(row == 0, mean, rstd)
    mean, rstd = mean[0:1], rstd[0:1]
    gain, shift = gain_ref[...], shift_ref[...]

    for t in range(t_n):
        for r in range(r_n):
            at = pl.ds((t * r_n + r) * w_n, w_n)
            hat = (lat_ref[t, r].astype(F32) - mean) * rstd
            pre = hat * gain + shift
            sig = jax.nn.sigmoid(pre)
            act = pre * sig
            hats[at, :] = hat
            slope[at, :] = sig * (1.0 + pre * (1.0 - sig))
            acts[at, 0:c_n] = before(act, True).astype(BF16)
            acts[at, c_n : 2 * c_n] = act.astype(BF16)
            acts[at, 2 * c_n :] = after(act, True).astype(BF16)

    def source(f, r):
        if 0 <= r < r_n:
            return (grad_ref[f, r] if f < t_n else halo_ref[f - t_n, r]).astype(F32)
        refs = edge_refs if f < t_n else corner_refs
        ref = refs[0] if r < 0 else refs[-1]
        return ref[f % t_n].astype(F32) * ((1.0 - top) if r < 0 else (1.0 - bottom))

    for j in range(3):
        for r in range(r_n):
            frame = []
            for f in range(t_n + 2):
                value = source(f, r + 1 - j)
                if j == 0 and r == 0:
                    value = value + source(f, 0) * top
                if j == 2 and r == r_n - 1:
                    value = value + source(f, r_n - 1) * bottom
                frame.append(value)
            for i in range(3):
                lanes = pl.ds((i * 3 + j) * c_n, c_n)
                for t in range(t_n):
                    value = frame[t + 2 - i]
                    if t == 0 and i < 2:
                        value = value + first * (frame[0] + frame[1] if i == 0 else frame[0])
                    fold[pl.ds((t * r_n + r) * w_n, w_n), lanes] = value.astype(BF16)

    product = lax.dot_general(
        acts[...], fold[...], (((0,), (0,)), ((), ())), preferred_element_type=F32
    )
    for ij in range(9):
        sums[pl.ds(ij * 3 * c_n, 3 * c_n), :] = product[:, ij * c_n : (ij + 1) * c_n]
    share = keep_ref.shape[0]
    if sums.shape[0] > 27 * c_n:
        sums[27 * c_n :, :] = jnp.zeros((sums.shape[0] - 27 * c_n, c_n), F32)
    keep_ref[...] = sums[pl.ds(h * share, share), :]
    for s, ref in enumerate(send_refs, 1):
        ref[0:share] = sums[pl.ds((h ^ s) * share, share), :].astype(BF16)

    for ij in range(9):
        weight[:, ij * c_n : (ij + 1) * c_n] = kernel_ref[ij // 3, ij % 3]
    total_a = jnp.zeros((8, c_n), F32)
    total_b = jnp.zeros((8, c_n), F32)
    for t in range(t_n):
        back = lax.dot_general(
            fold[pl.ds(t * r_n * w_n, r_n * w_n), :], weight[...], (((1,), (1,)), ((), ())),
            preferred_element_type=F32,
        )
        for r in range(r_n):
            slab = back[r * w_n : (r + 1) * w_n]
            low, mid, high = (slab[:, k * c_n : (k + 1) * c_n] for k in range(3))
            col = lax.broadcasted_iota(jnp.int32, low.shape, 0)
            dact = (
                mid + after(low, False) + before(high, False)
                + jnp.where(col == 0, low, 0.0) + jnp.where(col == w_n - 1, high, 0.0)
            )
            at = pl.ds((t * r_n + r) * w_n, w_n)
            dpre = dact * slope[at, :]
            dpre_ref[t, r] = dpre
            total_a += jnp.sum((dpre * hats[at, :]).reshape(w_n // 8, 8, c_n), axis=0)
            total_b += jnp.sum(dpre.reshape(w_n // 8, 8, c_n), axis=0)
    total_a = jnp.sum(total_a, axis=0, keepdims=True)
    total_b = jnp.sum(total_b, axis=0, keepdims=True)
    table = jnp.where(row == 0, bias_ref[...], jnp.where(row == 1, total_a, jnp.where(row == 2, total_b, 0.0)))
    table_ref[...] = table
    for ref in send_refs:
        ref[share:] = packed(table)


def first_sum_body(n_h, n_dp, keep_ref, table_ref, *rest):
    got, (own_ref, out_table), sends = rest[: n_h - 1], rest[n_h - 1 : n_h + 1], rest[n_h + 1 : -1]
    total = rest[-1]
    share, piece = keep_ref.shape[0], own_ref.shape[0]
    value = keep_ref[...]
    for ref in got:
        value = value + ref[0:share].astype(F32)
    total[...] = value
    table = tree([unpacked(packed(table_ref[...]))] + [unpacked(ref[share:]) for ref in got])
    out_table[...] = table
    me = lax.axis_index("dp")
    own_ref[...] = total[pl.ds(me * piece, piece), :]
    for s, ref in enumerate(sends, 1):
        ref[0:piece] = total[pl.ds((me ^ s) * piece, piece), :].astype(BF16)
        ref[piece:] = packed(table)


def second_sum_body(own_ref, table_ref, *rest):
    got, out_ref = rest[:-1], rest[-1]
    piece = own_ref.shape[0]
    value = own_ref[...]
    for ref in got:
        value = value + ref[0:piece].astype(F32)
    out_ref[0:piece] = value.astype(BF16)
    own = unpacked(packed(table_ref[...]))
    table = tree([own] + [unpacked(ref[piece:]) for ref in got])
    row = lax.broadcasted_iota(jnp.int32, table.shape, 0)
    kept = jnp.where(row == 0, table, jnp.where(row < 3, own, pltpu.roll(table, 2, 0)))
    out_ref[piece:] = packed(kept)


def pair_sum_body(a_ref, b_ref, out_ref):
    piece = a_ref.shape[0] - TAB
    out_ref[0:piece] = (a_ref[0:piece].astype(F32) + b_ref[0:piece].astype(F32)).astype(BF16)
    out_ref[piece:] = packed(unpacked(a_ref[piece:]) + unpacked(b_ref[piece:]))


def last_sum_body(a_ref, b_ref, out_ref, table_ref):
    piece = out_ref.shape[0]
    out_ref[...] = (a_ref[0:piece].astype(F32) + b_ref[0:piece].astype(F32)).astype(BF16)
    table_ref[...] = unpacked(a_ref[piece:]) + unpacked(b_ref[piece:])


def gather_body(own_ref, *rest):
    got, out_ref = rest[:-1], rest[-1]
    piece = own_ref.shape[0]
    me = lax.axis_index("dp")
    for s, ref in enumerate((own_ref, *got)):
        out_ref[pl.ds((me ^ s) * piece, piece), :] = ref[...]


def spread_body(own_ref, *rest):
    got, out_ref = rest[:-1], rest[-1]
    share, rows = own_ref.shape[0], out_ref.shape[0]
    h = lax.axis_index("height")
    for s, ref in enumerate((own_ref, *got)):
        for q in range(1 + len(got)):

            def put(ref=ref, q=q):
                count = min(share, rows - q * share)
                out_ref[q * share : q * share + count] = ref[0:count].astype(F32)

            pl.when((h ^ s) == q)(put)


def forward_body(
    n_edge, n_h,
    lat_ref, past_ref, norm_ref, kernel_ref, gain_ref, shift_ref, offset_ref, *rest,
):
    edge_refs, corner_refs, rest = rest[:n_edge], rest[n_edge : 2 * n_edge], rest[2 * n_edge :]
    out_ref, acts, slabs, weight, wide = rest
    t_n, r_n, w_n, c_n = lat_ref.shape
    h = lax.axis_index("height")
    mean, rstd = norm_ref[0:1], norm_ref[1:2]
    gain, shift = gain_ref[...], shift_ref[...]

    def silu(x):
        pre = (x.astype(F32) - mean) * rstd * gain + shift
        return (pre * jax.nn.sigmoid(pre)).astype(BF16)

    def act_of(f, r):
        if 0 <= r < r_n:
            return silu(past_ref[f, r] if f < 2 else lat_ref[f - 2, r])
        refs = corner_refs if f < 2 else edge_refs
        return silu((refs[0] if r < 0 else refs[-1])[f % 2])

    for f in range(t_n + 2):
        for r in range(-1, r_n + 1):
            acts[f, r + 1] = act_of(f, r)

    @pl.when(lax.axis_index("tm") == 0)
    def _():
        for f in range(2):
            for r in range(r_n + 2):
                acts[f, r] = acts[2, r]

    @pl.when(h == 0)
    def _():
        for f in range(t_n + 2):
            acts[f, 0] = acts[f, 1]

    @pl.when(h == n_h - 1)
    def _():
        for f in range(t_n + 2):
            acts[f, r_n + 1] = acts[f, r_n]

    for ij in range(9):
        i, j = ij // 3, ij % 3
        for k in range(3):
            weight[ij * c_n : (ij + 1) * c_n, k * c_n : (k + 1) * c_n] = kernel_ref[i, j, k * c_n : (k + 1) * c_n, :]
        for t in range(t_n):
            for r in range(r_n):
                slabs[(t * r_n + r) * w_n : (t * r_n + r + 1) * w_n, ij * c_n : (ij + 1) * c_n] = acts[t + i, r + j]
    offset = offset_ref[...]
    for t in range(t_n):
        value = jnp.dot(slabs[pl.ds(t * r_n * w_n, r_n * w_n), :], weight[...], preferred_element_type=F32)
        for r in range(r_n):
            slab = value[r * w_n : (r + 1) * w_n]
            low, mid, high = (slab[:, k * c_n : (k + 1) * c_n] for k in range(3))
            conv = before(low, True) + mid + after(high, True) + offset
            slot = r % 2
            conv = conv.astype(BF16).astype(F32)
            wide[slot, pl.ds(0, w_n, stride=2), :] = conv
            wide[slot, pl.ds(1, w_n, stride=2), :] = conv
            both = wide[slot].astype(BF16)
            out_ref[t, 2 * r] = both
            out_ref[t, 2 * r + 1] = both


def last_body(cells, dpre_ref, lat_ref, norm_ref, table_ref, gain_ref, out_ref, bias_ref, gains_ref, shifts_ref):
    t_n, r_n, w_n, c_n = lat_ref.shape
    table, gain = table_ref[...], gain_ref[...]
    mean, rstd = norm_ref[0:1], norm_ref[1:2]
    scale = 1.0 / (cells * (c_n // GROUPS))
    means = group_sum(table * gain) * scale
    mean_b, mean_a = means[1:2], means[2:3]
    bias_ref[...] = table[0:1]
    gains_ref[...] = table[3:4]
    shifts_ref[...] = table[4:5]
    for t in range(t_n):
        for r in range(r_n):
            hat = (lat_ref[t, r].astype(F32) - mean) * rstd
            out_ref[t, r] = (rstd * (dpre_ref[t, r] * gain - mean_a - hat * mean_b)).astype(BF16)


def local(latents, cotangent, group_norm_gain, group_norm_bias, kernel, kernel_bias):
    lat, cot = latents[0], cotangent[0]
    t_n, r_n, w_n, c_n = lat.shape
    n_dp, n_t, n_h = (lax.axis_size(axis) for axis in ("dp", "tm", "height"))
    n_edge = 1 if n_h == 2 else 2
    gain, shift, offset = (v.reshape(1, c_n) for v in (group_norm_gain, group_norm_bias, kernel_bias))
    grid = (t_n, r_n, w_n, c_n)
    edge = (t_n, w_n, c_n)
    rows = 27 * c_n
    unit = n_h * n_dp * 16
    total = -(-rows // unit) * unit
    share, piece = total // n_h, total // (n_h * n_dp)

    grad, bias_part, *edge_list = call(
        functools.partial(fold_body, n_edge),
        [shape(grid, BF16), shape((8, c_n), F32)] + [shape(edge, BF16)] * n_edge,
        cot,
        scratch=[pltpu.VMEM((2, 2 * w_n, c_n), F32)],
    )
    (stats,) = call(stats_body, [shape((8, c_n), F32)], lat)
    halo = moved(grad, 1, 0)
    edge_rows = facing(edge_list, 0)
    corner_rows = facing(edge_list, 1)

    rounds = [("height", 1 << i) for i in range(n_h.bit_length() - 1)]
    rounds += [("tm", 1 << i) for i in range(n_t.bit_length() - 1)]
    cells = t_n * r_n * w_n
    other = None
    for axis, distance in rounds:
        if other is not None:
            gap = stats[0:1] - other[0:1]
            stats = jnp.concatenate(
                [
                    (stats[0:1] + other[0:1]) * 0.5,
                    stats[1:2] + other[1:2] + gap * gap * (cells / 4),
                    jnp.zeros((6, c_n), F32),
                ]
            )
        other = swap(stats, axis, distance)
        cells = cells * 2

    keep, table, dpre, norm, *sends = call(
        functools.partial(main_body, n_edge, cells, n_h),
        [shape((share, c_n), F32), shape((8, c_n), F32), shape(grid, F32), shape((8, c_n), F32)]
        + [shape((share + TAB, c_n), BF16)] * (n_h - 1),
        lat, stats, other, grad, halo, kernel, gain, shift, bias_part, *edge_rows, *corner_rows,
        scratch=[
            pltpu.VMEM((t_n * r_n * w_n, 3 * c_n), BF16),
            pltpu.VMEM((t_n * r_n * w_n, 9 * c_n), BF16),
            pltpu.VMEM((3 * c_n, 9 * c_n), BF16),
            pltpu.VMEM((t_n * r_n * w_n, c_n), F32),
            pltpu.VMEM((t_n * r_n * w_n, c_n), F32),
            pltpu.VMEM((total, c_n), F32),
        ],
        flops=4 * 27 * t_n * r_n * w_n * c_n * c_n,
    )

    past = moved(lat, -1, 0)
    if n_edge == 1:
        row = jnp.where(lax.axis_index("height") == 0, r_n - 1, 0)
        lat_edges = [lax.dynamic_index_in_dim(lat, row, 1, keepdims=False)]
    else:
        lat_edges = [lat[:, r_n - 1], lat[:, 0]]
    lat_rows = facing(lat_edges, 0)
    lat_corners = facing(lat_edges, -1)

    got = [swap(send, "height", s) for s, send in enumerate(sends, 1)]
    own, table, *sends = call(
        functools.partial(first_sum_body, n_h, n_dp),
        [shape((piece, c_n), F32), shape((8, c_n), F32)] + [shape((piece + TAB, c_n), BF16)] * (n_dp - 1),
        keep, table, *got,
        scratch=[pltpu.VMEM((share, c_n), F32)],
    )
    got = [swap(send, "dp", s) for s, send in enumerate(sends, 1)]
    (part,) = call(second_sum_body, [shape((piece + TAB, c_n), BF16)], own, table, *got)
    distance = 1
    while distance < n_t:
        other = swap(part, "tm", distance)
        distance *= 2
        if distance < n_t:
            (part,) = call(pair_sum_body, [shape((piece + TAB, c_n), BF16)], part, other)
    part, table = call(last_sum_body, [shape((piece, c_n), BF16), shape((8, c_n), F32)], part, other)
    got = [swap(part, "dp", s) for s in range(1, n_dp)]
    (half,) = call(gather_body, [shape((share, c_n), BF16)], part, *got)
    got = [swap(half, "height", s) for s in range(1, n_h)]
    (kernel_grad,) = call(spread_body, [shape((rows, c_n), F32)], half, *got)

    (upsampled,) = call(
        functools.partial(forward_body, n_edge, n_h),
        [shape(cot.shape, BF16)],
        lat, past, norm, kernel, gain, shift, offset, *lat_rows, *lat_corners,
        scratch=[
            pltpu.VMEM((t_n + 2, r_n + 2, w_n, c_n), BF16),
            pltpu.VMEM((t_n * r_n * w_n, 9 * c_n), BF16),
            pltpu.VMEM((9 * c_n, 3 * c_n), BF16),
            pltpu.VMEM((2, 2 * w_n, c_n), F32),
        ],
        flops=2 * 27 * t_n * r_n * w_n * c_n * c_n,
    )
    latent_gradient, bias_grad, gain_grad, shift_grad = call(
        functools.partial(last_body, cells),
        [shape(grid, BF16)] + [shape((1, c_n), F32)] * 3,
        dpre, lat, norm, table, gain,
    )
    return (
        upsampled[None],
        latent_gradient[None],
        kernel_grad.reshape(kernel.shape),
        bias_grad.reshape(c_n),
        gain_grad.reshape(c_n),
        shift_grad.reshape(c_n),
    )


def solution(mesh):
    split = P("dp", "tm", "height", None, None)
    return jax.shard_map(
        local,
        mesh=mesh,
        in_specs=(split, split, P(), P(), P(), P()),
        out_specs=(split, split, P(), P(), P(), P()),
        check_vma=False,
    )
```

```python
import functools
import math

import jax
import jax.numpy as jnp
from jax import lax
from jax.experimental import pallas as pl
from jax.experimental.pallas import tpu as pltpu
from jax.sharding import PartitionSpec as P

GROUPS = 32
F32 = jnp.float32
BF16 = jnp.bfloat16
TAB = 32
VMEM = pl.BlockSpec(memory_space=pltpu.VMEM)


def call(body, outs, *args, scratch=(), flops=1_000_000, room=2 << 20):
    moved = sum(a.size * a.dtype.itemsize for a in (*args, *outs))
    held = sum(math.prod(s.shape) * jnp.dtype(s.dtype).itemsize for s in scratch)
    return pl.pallas_call(
        body,
        out_shape=tuple(outs),
        in_specs=[VMEM] * len(args),
        out_specs=tuple([VMEM] * len(outs)),
        scratch_shapes=list(scratch),
        compiler_params=pltpu.CompilerParams(vmem_limit_bytes=moved + held + room),
        cost_estimate=pl.CostEstimate(flops=flops, bytes_accessed=moved, transcendentals=0),
    )(*args)


def shape(dims, dtype):
    return jax.ShapeDtypeStruct(dims, dtype)


def swap(block, axis, distance):
    count = lax.axis_size(axis)
    return lax.ppermute(block, axis, [(i, i ^ distance) for i in range(count)])


def moved(block, frames, rows):
    n_t, n_h = lax.axis_size("tm"), lax.axis_size("height")
    route = []
    for t in range(n_t):
        for h in range(n_h):
            if 0 <= t + frames < n_t and 0 <= h + rows < n_h:
                route.append(((t + frames) * n_h + h + rows, t * n_h + h))
    return lax.ppermute(block, ("tm", "height"), route)


def across(block, frames):
    n_t = lax.axis_size("tm")
    route = []
    for t in range(n_t):
        for h in range(2):
            if 0 <= t + frames < n_t:
                route.append(((t + frames) * 2 + 1 - h, t * 2 + h))
    return lax.ppermute(block, ("tm", "height"), route)


def facing(edges, frames):
    if len(edges) == 1:
        other = across(edges[0], frames)
        return [other]
    return [moved(edges[0], frames, -1), moved(edges[1], frames, 1)]


def tree(values):
    while len(values) > 1:
        values = [values[i] + values[i + 1] for i in range(0, len(values), 2)]
    return values[0]


def group_sum(x):
    lane = lax.broadcasted_iota(jnp.int32, x.shape, 1)
    n = x.shape[1]
    x = x + jnp.where(lane % 2 == 0, pltpu.roll(x, n - 1, 1), pltpu.roll(x, 1, 1))
    return x + jnp.where(lane % 4 < 2, pltpu.roll(x, n - 2, 1), pltpu.roll(x, 2, 1))


def packed(table):
    high = table.astype(BF16).astype(F32)
    rest = table - high
    mid = rest.astype(BF16).astype(F32)
    low = (rest - mid).astype(BF16).astype(F32)
    return jnp.concatenate([high, mid, low, jnp.zeros_like(low)], axis=0).astype(BF16)


def unpacked(rows):
    rows = rows.astype(F32)
    return (rows[0:8] + rows[8:16]) + rows[16:24]


def before(x, edge):
    row = lax.broadcasted_iota(jnp.int32, x.shape, 0)
    return jnp.where(row == 0, x if edge else 0.0, pltpu.roll(x, 1, 0))


def after(x, edge):
    row = lax.broadcasted_iota(jnp.int32, x.shape, 0)
    return jnp.where(row == x.shape[0] - 1, x if edge else 0.0, pltpu.roll(x, x.shape[0] - 1, 0))


def fold_body(edge_n, cot_ref, out_ref, bias_ref, *rest):
    edge_refs, wide = rest[:edge_n], rest[edge_n]
    t_n, r2, w2, c_n = cot_ref.shape
    r_n, w_n = r2 // 2, w2 // 2
    total = jnp.zeros((8, c_n), F32)
    for t in range(t_n):
        for r in range(r_n):
            slot = (t * r_n + r) % 2
            wide[slot] = cot_ref[t, 2 * r].astype(F32) + cot_ref[t, 2 * r + 1].astype(F32)
            value = wide[slot, pl.ds(0, w_n, stride=2), :] + wide[slot, pl.ds(1, w_n, stride=2), :]
            total += jnp.sum(value.reshape(w_n // 8, 8, c_n), axis=0)
            out_ref[t, r] = value.astype(BF16)
    bias_ref[...] = jnp.broadcast_to(jnp.sum(total, axis=0, keepdims=True), (8, c_n))
    for ref, row in zip(edge_refs, facing_rows(edge_n, r_n)):
        ref[...] = out_ref[:, row]


def facing_rows(edge_n, r_n):
    if edge_n == 1:
        return [jnp.where(lax.axis_index("height") == 0, r_n - 1, 0)]
    return [r_n - 1, 0]


def stats_body(edge_n, lat_ref, grad_ref, out_ref, *edge_refs):
    t_n, r_n, w_n, c_n = lat_ref.shape
    total = jnp.zeros((8, c_n), F32)
    for t in range(t_n):
        for r in range(r_n):
            total += jnp.sum(lat_ref[t, r].astype(F32).reshape(w_n // 8, 8, c_n), axis=0)
    mean = jnp.sum(total, axis=0, keepdims=True) / (t_n * r_n * w_n)
    square = jnp.zeros((8, c_n), F32)
    for t in range(t_n):
        for r in range(r_n):
            x = (lat_ref[t, r].astype(F32) - mean).reshape(w_n // 8, 8, c_n)
            square += jnp.sum(x * x, axis=0)
    square = jnp.sum(square, axis=0, keepdims=True)
    row = lax.broadcasted_iota(jnp.int32, (8, c_n), 0)
    stats = jnp.where(row == 0, mean, jnp.where(row == 1, square, 0.0))
    out_ref[...] = stats
    for ref, row in zip(edge_refs, facing_rows(edge_n, r_n)):
        for t in range(t_n):
            ref[pl.ds(t * w_n, w_n), :] = lat_ref[t, row]
            ref[pl.ds((t_n + t) * w_n, w_n), :] = grad_ref[t, row]
        ref[pl.ds(2 * t_n * w_n, TAB), :] = packed(stats)


def merged(a, b, cells):
    gap = a[0:1] - b[0:1]
    return (a[0:1] + b[0:1]) * 0.5, a[1:2] + b[1:2] + gap * gap * (cells / 4)


def merge_body(cells, a_ref, b_ref, out_ref):
    a = a_ref[...]
    if b_ref.shape[0] == 8:
        b = b_ref[...]
    else:
        a = unpacked(packed(a))
        b = unpacked(b_ref[b_ref.shape[0] - TAB :])
    mean, square = merged(a, b, cells)
    row = lax.broadcasted_iota(jnp.int32, a.shape, 0)
    out_ref[...] = jnp.where(row == 0, mean, jnp.where(row == 1, square, 0.0))


def back_body(n_edge, n_h, lat_ref, stats_ref, grad_ref, halo_ref, kernel_ref, *rest):
    edge_refs, corner_refs, rest = rest[:n_edge], rest[n_edge : 2 * n_edge], rest[2 * n_edge :]
    fold, dact_ref, lead_ref, weight = rest
    t_n, r_n, w_n, c_n = lat_ref.shape
    h = lax.axis_index("height")
    top = (h == 0).astype(F32)
    bottom = (h == n_h - 1).astype(F32)
    first = (lax.axis_index("tm") == 0).astype(F32)

    for t in range(t_n):
        for r in range(r_n):
            lead_ref[t, r] = lat_ref[t, r]
        for e, ref in enumerate(edge_refs):
            lead_ref[t, r_n + e] = ref[pl.ds(t * w_n, w_n), :]

    def source(f, r):
        if 0 <= r < r_n:
            return (grad_ref[f, r] if f < t_n else halo_ref[f - t_n, r]).astype(F32)
        which = 0 if r < 0 else -1
        if f < t_n:
            value = edge_refs[which][pl.ds((t_n + f) * w_n, w_n), :]
        else:
            value = corner_refs[which][f - t_n]
        return value.astype(F32) * ((1.0 - top) if r < 0 else (1.0 - bottom))

    for j in range(3):
        for r in range(r_n):
            frame = []
            for f in range(t_n + 2):
                value = source(f, r + 1 - j)
                if j == 0 and r == 0:
                    value = value + source(f, 0) * top
                if j == 2 and r == r_n - 1:
                    value = value + source(f, r_n - 1) * bottom
                frame.append(value)
            for i in range(3):
                lanes = pl.ds((i * 3 + j) * c_n, c_n)
                for t in range(t_n):
                    value = frame[t + 2 - i]
                    if t == 0 and i < 2:
                        value = value + first * (frame[0] + frame[1] if i == 0 else frame[0])
                    fold[pl.ds((t * r_n + r) * w_n, w_n), lanes] = value.astype(BF16)

    for ij in range(9):
        weight[:, ij * c_n : (ij + 1) * c_n] = kernel_ref[ij // 3, ij % 3]
    for t in range(t_n):
        back = lax.dot_general(
            fold[pl.ds(t * r_n * w_n, r_n * w_n), :], weight[...], (((1,), (1,)), ((), ())),
            preferred_element_type=F32,
        )
        for r in range(r_n):
            slab = back[r * w_n : (r + 1) * w_n]
            low, mid, high = (slab[:, k * c_n : (k + 1) * c_n] for k in range(3))
            col = lax.broadcasted_iota(jnp.int32, low.shape, 0)
            dact_ref[t, r] = (
                mid + after(low, False) + before(high, False)
                + jnp.where(col == 0, low, 0.0) + jnp.where(col == w_n - 1, high, 0.0)
            )


def main_body(
    cells, n_h,
    lat_ref, mine_ref, other_ref, fold_ref, dact_ref, gain_ref, shift_ref, bias_ref, *rest,
):
    keep_ref, table_ref, dpre_ref, norm_ref = rest[:4]
    send_refs, (acts, sums) = rest[4 : 3 + n_h], rest[3 + n_h :]
    t_n, r_n, w_n, c_n = lat_ref.shape
    h = lax.axis_index("height")

    channel_mean, square = merged(mine_ref[...], other_ref[...], cells)
    channel_mean = jnp.broadcast_to(channel_mean, (8, c_n))
    size = c_n // GROUPS
    mean = group_sum(channel_mean) * (1.0 / size)
    off = channel_mean - mean
    var = group_sum(jnp.broadcast_to(square, (8, c_n)) + off * off * cells) * (1.0 / (cells * size))
    rstd = lax.rsqrt(var + 1e-06)
    row = lax.broadcasted_iota(jnp.int32, (8, c_n), 0)
    norm_ref[...] = jnp.where(row == 0, mean, rstd)
    mean, rstd = mean[0:1], rstd[0:1]
    gain, shift = gain_ref[...], shift_ref[...]

    total_a = jnp.zeros((8, c_n), F32)
    total_b = jnp.zeros((8, c_n), F32)
    for t in range(t_n):
        for r in range(r_n):
            at = pl.ds((t * r_n + r) * w_n, w_n)
            hat = (lat_ref[t, r].astype(F32) - mean) * rstd
            pre = hat * gain + shift
            sig = jax.nn.sigmoid(pre)
            act = pre * sig
            acts[at, 0:c_n] = before(act, True).astype(BF16)
            acts[at, c_n : 2 * c_n] = act.astype(BF16)
            acts[at, 2 * c_n :] = after(act, True).astype(BF16)
            dpre = dact_ref[t, r] * sig * (1.0 + pre * (1.0 - sig))
            dpre_ref[t, r] = dpre
            total_a += jnp.sum((dpre * hat).reshape(w_n // 8, 8, c_n), axis=0)
            total_b += jnp.sum(dpre.reshape(w_n // 8, 8, c_n), axis=0)
    total_a = jnp.sum(total_a, axis=0, keepdims=True)
    total_b = jnp.sum(total_b, axis=0, keepdims=True)
    table = jnp.where(row == 0, bias_ref[...], jnp.where(row == 1, total_a, jnp.where(row == 2, total_b, 0.0)))
    table_ref[...] = table

    product = lax.dot_general(
        acts[...], fold_ref[...], (((0,), (0,)), ((), ())), preferred_element_type=F32
    )
    for ij in range(9):
        sums[pl.ds(ij * 3 * c_n, 3 * c_n), :] = product[:, ij * c_n : (ij + 1) * c_n]
    share = keep_ref.shape[0]
    if sums.shape[0] > 27 * c_n:
        sums[27 * c_n :, :] = jnp.zeros((sums.shape[0] - 27 * c_n, c_n), F32)
    keep_ref[...] = sums[pl.ds(h * share, share), :]
    for s, ref in enumerate(send_refs, 1):
        ref[0:share] = sums[pl.ds((h ^ s) * share, share), :].astype(BF16)
        ref[share:] = packed(table)


def first_sum_body(n_h, n_dp, keep_ref, table_ref, *rest):
    got, (own_ref, out_table), sends = rest[: n_h - 1], rest[n_h - 1 : n_h + 1], rest[n_h + 1 : -1]
    total = rest[-1]
    share, piece = keep_ref.shape[0], own_ref.shape[0]
    value = keep_ref[...]
    for ref in got:
        value = value + ref[0:share].astype(F32)
    total[...] = value
    table = tree([unpacked(packed(table_ref[...]))] + [unpacked(ref[share:]) for ref in got])
    out_table[...] = table
    me = lax.axis_index("dp")
    own_ref[...] = total[pl.ds(me * piece, piece), :]
    for s, ref in enumerate(sends, 1):
        ref[0:piece] = total[pl.ds((me ^ s) * piece, piece), :].astype(BF16)
        ref[piece:] = packed(table)


def second_sum_body(own_ref, table_ref, token_ref, *rest):
    got, out_ref = rest[:-1], rest[-1]
    piece = own_ref.shape[0]
    value = own_ref[...]
    for ref in got:
        value = value + ref[0:piece].astype(F32)
    out_ref[0:piece] = value.astype(BF16)
    own = unpacked(packed(table_ref[...]))
    table = tree([own] + [unpacked(ref[piece:]) for ref in got])
    row = lax.broadcasted_iota(jnp.int32, table.shape, 0)
    kept = jnp.where(row == 0, table, jnp.where(row < 3, own, pltpu.roll(table, 2, 0)))
    out_ref[piece:] = packed(kept)


def pair_sum_body(a_ref, b_ref, out_ref):
    piece = a_ref.shape[0] - TAB
    out_ref[0:piece] = (a_ref[0:piece].astype(F32) + b_ref[0:piece].astype(F32)).astype(BF16)
    out_ref[piece:] = packed(unpacked(a_ref[piece:]) + unpacked(b_ref[piece:]))


def last_sum_body(a_ref, b_ref, out_ref, table_ref):
    piece = out_ref.shape[0]
    out_ref[...] = (a_ref[0:piece].astype(F32) + b_ref[0:piece].astype(F32)).astype(BF16)
    table_ref[...] = unpacked(a_ref[piece:]) + unpacked(b_ref[piece:])


def gather_body(token_ref, own_ref, *rest):
    got, out_ref = rest[:-1], rest[-1]
    piece = own_ref.shape[0]
    me = lax.axis_index("dp")
    for s, ref in enumerate((own_ref, *got)):
        out_ref[pl.ds((me ^ s) * piece, piece), :] = ref[...]


def spread_body(own_ref, *rest):
    got, out_ref = rest[:-1], rest[-1]
    share, rows = own_ref.shape[0], out_ref.shape[0]
    h = lax.axis_index("height")
    for s, ref in enumerate((own_ref, *got)):
        for q in range(1 + len(got)):

            def put(ref=ref, q=q):
                count = min(share, rows - q * share)
                out_ref[q * share : q * share + count] = ref[0:count].astype(F32)

            pl.when((h ^ s) == q)(put)


def forward_body(
    n_edge, n_h,
    lat_ref, past_ref, norm_ref, kernel_ref, gain_ref, shift_ref, offset_ref, after_ref, *rest,
):
    edge_refs, rest = rest[:n_edge], rest[n_edge:]
    out_ref, token_ref, acts, slabs, weight, wide = rest
    token_ref[...] = jnp.zeros_like(token_ref)
    t_n, r_n, w_n, c_n = lat_ref.shape
    h = lax.axis_index("height")
    mean, rstd = norm_ref[0:1], norm_ref[1:2]
    gain, shift = gain_ref[...], shift_ref[...]

    def silu(x):
        pre = (x.astype(F32) - mean) * rstd * gain + shift
        return (pre * jax.nn.sigmoid(pre)).astype(BF16)

    def act_of(f, r):
        if 0 <= r < r_n:
            return silu(past_ref[f, r] if f < 2 else lat_ref[f - 2, r])
        which = 0 if r < 0 else n_edge - 1
        if f < 2:
            return silu(past_ref[f, r_n + which])
        return silu(edge_refs[which][pl.ds((f - 2) * w_n, w_n), :])

    for f in range(t_n + 2):
        for r in range(-1, r_n + 1):
            acts[f, r + 1] = act_of(f, r)

    @pl.when(lax.axis_index("tm") == 0)
    def _():
        for f in range(2):
            for r in range(r_n + 2):
                acts[f, r] = acts[2, r]

    @pl.when(h == 0)
    def _():
        for f in range(t_n + 2):
            acts[f, 0] = acts[f, 1]

    @pl.when(h == n_h - 1)
    def _():
        for f in range(t_n + 2):
            acts[f, r_n + 1] = acts[f, r_n]

    for ij in range(9):
        i, j = ij // 3, ij % 3
        for k in range(3):
            weight[ij * c_n : (ij + 1) * c_n, k * c_n : (k + 1) * c_n] = kernel_ref[i, j, k * c_n : (k + 1) * c_n, :]
        for t in range(t_n):
            for r in range(r_n):
                slabs[(t * r_n + r) * w_n : (t * r_n + r + 1) * w_n, ij * c_n : (ij + 1) * c_n] = acts[t + i, r + j]
    offset = offset_ref[...]
    for t in range(t_n):
        value = jnp.dot(slabs[pl.ds(t * r_n * w_n, r_n * w_n), :], weight[...], preferred_element_type=F32)
        for r in range(r_n):
            slab = value[r * w_n : (r + 1) * w_n]
            low, mid, high = (slab[:, k * c_n : (k + 1) * c_n] for k in range(3))
            conv = before(low, True) + mid + after(high, True) + offset
            slot = r % 2
            conv = conv.astype(BF16).astype(F32)
            wide[slot, pl.ds(0, w_n, stride=2), :] = conv
            wide[slot, pl.ds(1, w_n, stride=2), :] = conv
            both = wide[slot].astype(BF16)
            out_ref[t, 2 * r] = both
            out_ref[t, 2 * r + 1] = both


def last_body(cells, dpre_ref, lat_ref, norm_ref, table_ref, gain_ref, out_ref, bias_ref, gains_ref, shifts_ref):
    t_n, r_n, w_n, c_n = lat_ref.shape
    table, gain = table_ref[...], gain_ref[...]
    mean, rstd = norm_ref[0:1], norm_ref[1:2]
    scale = 1.0 / (cells * (c_n // GROUPS))
    means = group_sum(table * gain) * scale
    mean_b, mean_a = means[1:2], means[2:3]
    bias_ref[...] = table[0:1]
    gains_ref[...] = table[3:4]
    shifts_ref[...] = table[4:5]
    for t in range(t_n):
        for r in range(r_n):
            hat = (lat_ref[t, r].astype(F32) - mean) * rstd
            out_ref[t, r] = (rstd * (dpre_ref[t, r] * gain - mean_a - hat * mean_b)).astype(BF16)


def local(latents, cotangent, group_norm_gain, group_norm_bias, kernel, kernel_bias):
    lat, cot = latents[0], cotangent[0]
    t_n, r_n, w_n, c_n = lat.shape
    n_dp, n_t, n_h = (lax.axis_size(axis) for axis in ("dp", "tm", "height"))
    n_edge = 1 if n_h == 2 else 2
    gain, shift, offset = (v.reshape(1, c_n) for v in (group_norm_gain, group_norm_bias, kernel_bias))
    grid = (t_n, r_n, w_n, c_n)
    edge = (t_n, w_n, c_n)
    small = shape((8, c_n), F32)
    rows = 27 * c_n
    unit = n_h * n_dp * 16
    total = -(-rows // unit) * unit
    share, piece = total // n_h, total // (n_h * n_dp)

    grad, bias_part, *corners = call(
        functools.partial(fold_body, n_edge),
        [shape(grid, BF16), small] + [shape(edge, BF16)] * n_edge,
        cot,
        scratch=[pltpu.VMEM((2, 2 * w_n, c_n), F32)],
    )
    halo = moved(grad, 1, 0)
    corner_rows = facing(corners, 1)
    stats, *edge_list = call(
        functools.partial(stats_body, n_edge),
        [small] + [shape((2 * t_n * w_n + TAB, c_n), BF16)] * n_edge,
        lat, grad,
    )
    edge_rows = facing(edge_list, 0)

    rounds = [("height", 1 << i) for i in range(n_h.bit_length() - 1)]
    rounds += [("tm", 1 << i) for i in range(n_t.bit_length() - 1)]
    cells = t_n * r_n * w_n
    other = None
    for axis, distance in rounds:
        if other is not None:
            (stats,) = call(functools.partial(merge_body, cells), [small], stats, other)
        if n_h == 2 and axis == "height":
            other = edge_rows[0]
        else:
            other = swap(stats, axis, distance)
        cells = cells * 2

    fold, dact, lead = call(
        functools.partial(back_body, n_edge, n_h),
        [shape((t_n * r_n * w_n, 9 * c_n), BF16), shape(grid, F32), shape((t_n, r_n + n_edge, w_n, c_n), BF16)],
        lat, stats, grad, halo, kernel, *edge_rows, *corner_rows,
        scratch=[pltpu.VMEM((3 * c_n, 9 * c_n), BF16)],
        room=6 << 20,
        flops=2 * 27 * t_n * r_n * w_n * c_n * c_n,
    )
    past = moved(lead, -1, 0)
    keep, table, dpre, norm, *sends = call(
        functools.partial(main_body, cells, n_h),
        [shape((share, c_n), F32), small, shape(grid, F32), small]
        + [shape((share + TAB, c_n), BF16)] * (n_h - 1),
        lat, stats, other, fold, dact, gain, shift, bias_part,
        scratch=[
            pltpu.VMEM((t_n * r_n * w_n, 3 * c_n), BF16),
            pltpu.VMEM((total, c_n), F32),
        ],
        room=8 << 20,
        flops=2 * 27 * t_n * r_n * w_n * c_n * c_n,
    )

    got = [swap(send, "height", s) for s, send in enumerate(sends, 1)]
    own, table, *sends = call(
        functools.partial(first_sum_body, n_h, n_dp),
        [shape((piece, c_n), F32), small] + [shape((piece + TAB, c_n), BF16)] * (n_dp - 1),
        keep, table, *got,
        scratch=[pltpu.VMEM((share, c_n), F32)],
    )
    got = [swap(send, "dp", s) for s, send in enumerate(sends, 1)]
    upsampled, token = call(
        functools.partial(forward_body, n_edge, n_h),
        [shape(cot.shape, BF16), small],
        lat, past, norm, kernel, gain, shift, offset, table, *edge_rows,
        scratch=[
            pltpu.VMEM((t_n + 2, r_n + 2, w_n, c_n), BF16),
            pltpu.VMEM((t_n * r_n * w_n, 9 * c_n), BF16),
            pltpu.VMEM((9 * c_n, 3 * c_n), BF16),
            pltpu.VMEM((2, 2 * w_n, c_n), F32),
        ],
        room=6 << 20,
        flops=2 * 27 * t_n * r_n * w_n * c_n * c_n,
    )
    (part,) = call(second_sum_body, [shape((piece + TAB, c_n), BF16)], own, table, token, *got)
    distance = 1
    while distance < n_t:
        other = swap(part, "tm", distance)
        distance *= 2
        if distance < n_t:
            (part,) = call(pair_sum_body, [shape((piece + TAB, c_n), BF16)], part, other)
    part, table = call(last_sum_body, [shape((piece, c_n), BF16), small], part, other)
    got = [swap(part, "dp", s) for s in range(1, n_dp)]
    latent_gradient, bias_grad, gain_grad, shift_grad = call(
        functools.partial(last_body, cells),
        [shape(grid, BF16)] + [shape((1, c_n), F32)] * 3,
        dpre, lat, norm, table, gain,
    )
    (half,) = call(gather_body, [shape((share, c_n), BF16)], shift_grad, part, *got)
    got = [swap(half, "height", s) for s in range(1, n_h)]
    (kernel_grad,) = call(spread_body, [shape((rows, c_n), F32)], half, *got)
    return (
        upsampled[None],
        latent_gradient[None],
        kernel_grad.reshape(kernel.shape),
        bias_grad.reshape(c_n),
        gain_grad.reshape(c_n),
        shift_grad.reshape(c_n),
    )


def solution(mesh):
    split = P("dp", "tm", "height", None, None)
    return jax.shard_map(
        local,
        mesh=mesh,
        in_specs=(split, split, P(), P(), P(), P()),
        out_specs=(split, split, P(), P(), P(), P()),
        check_vma=False,
    )
```

```python
import functools
import math

import jax
import jax.numpy as jnp
from jax import lax
from jax.experimental import pallas as pl
from jax.experimental.pallas import tpu as pltpu
from jax.sharding import PartitionSpec as P


GROUPS = 32
F32 = jnp.float32
BF16 = jnp.bfloat16
TAB = 32
VMEM = pl.BlockSpec(memory_space=pltpu.VMEM)


HBM = pl.BlockSpec(memory_space=pltpu.HBM)


def call(body, outs, *args, scratch=(), flops=1_000_000, room=2 << 20, far=(), far_out=(), alias=None):
    size = [a.size * a.dtype.itemsize for a in (*args, *outs)]
    out_of = {*far, *(len(args) + i for i in far_out)}
    near = sum(n for i, n in enumerate(size) if i not in out_of)
    held = sum(math.prod(s.shape) * jnp.dtype(s.dtype).itemsize for s in scratch if s.memory_space == pltpu.VMEM)
    return pl.pallas_call(
        body,
        out_shape=tuple(outs),
        in_specs=[HBM if i in far else VMEM for i in range(len(args))],
        out_specs=tuple(HBM if i in far_out else VMEM for i in range(len(outs))),
        scratch_shapes=list(scratch),
        input_output_aliases=alias or {},
        compiler_params=pltpu.CompilerParams(vmem_limit_bytes=near + held + room),
        cost_estimate=pl.CostEstimate(flops=flops, bytes_accessed=sum(size), transcendentals=0),
    )(*args)


def shape(dims, dtype):
    return jax.ShapeDtypeStruct(dims, dtype)


def swap(block, axis, distance):
    count = lax.axis_size(axis)
    return lax.ppermute(block, axis, [(i, i ^ distance) for i in range(count)])


def moved(block, frames, rows):
    n_t, n_h = lax.axis_size("tm"), lax.axis_size("height")
    route = []
    for t in range(n_t):
        for h in range(n_h):
            if 0 <= t + frames < n_t and 0 <= h + rows < n_h:
                route.append(((t + frames) * n_h + h + rows, t * n_h + h))
    return lax.ppermute(block, ("tm", "height"), route)


def across(block, frames):
    n_t = lax.axis_size("tm")
    route = []
    for t in range(n_t):
        for h in range(2):
            if 0 <= t + frames < n_t:
                route.append(((t + frames) * 2 + 1 - h, t * 2 + h))
    return lax.ppermute(block, ("tm", "height"), route)


def facing(edges, frames):
    if len(edges) == 1:
        other = across(edges[0], frames)
        return [other]
    return [moved(edges[0], frames, -1), moved(edges[1], frames, 1)]


def tree(values):
    while len(values) > 1:
        values = [values[i] + values[i + 1] for i in range(0, len(values), 2)]
    return values[0]


def group_sum(x):
    lane = lax.broadcasted_iota(jnp.int32, x.shape, 1)
    n = x.shape[1]
    x = x + jnp.where(lane % 2 == 0, pltpu.roll(x, n - 1, 1), pltpu.roll(x, 1, 1))
    return x + jnp.where(lane % 4 < 2, pltpu.roll(x, n - 2, 1), pltpu.roll(x, 2, 1))


def packed(table):
    high = table.astype(BF16).astype(F32)
    rest = table - high
    mid = rest.astype(BF16).astype(F32)
    low = (rest - mid).astype(BF16).astype(F32)
    return jnp.concatenate([high, mid, low, jnp.zeros_like(low)], axis=0).astype(BF16)


def unpacked(rows):
    rows = rows.astype(F32)
    return (rows[0:8] + rows[8:16]) + rows[16:24]


def before(x, edge):
    row = lax.broadcasted_iota(jnp.int32, x.shape, 0)
    return jnp.where(row == 0, x if edge else 0.0, pltpu.roll(x, 1, 0))


def after(x, edge):
    row = lax.broadcasted_iota(jnp.int32, x.shape, 0)
    return jnp.where(row == x.shape[0] - 1, x if edge else 0.0, pltpu.roll(x, x.shape[0] - 1, 0))


def facing_rows(edge_n, r_n):
    if edge_n == 1:
        return [jnp.where(lax.axis_index("height") == 0, r_n - 1, 0)]
    return [r_n - 1, 0]


def front_body(edge_n, cot_hbm, lat_hbm, lat_ref, grad_ref, bias_ref, stats_ref, *rest):
    edge_refs, corner_refs, (cot_ref, wide, cot_sem, lat_sem) = rest[:edge_n], rest[edge_n : 2 * edge_n], rest[2 * edge_n :]
    t_n, r_n, w_n, c_n = lat_ref.shape
    cot_copies = [
        pltpu.make_async_copy(
            cot_hbm.at[t, pl.ds(2 * r, 2)], cot_ref.at[t, pl.ds(2 * r, 2)], cot_sem.at[t * r_n + r]
        )
        for t in range(t_n)
        for r in range(r_n)
    ]
    lat_copies = [pltpu.make_async_copy(lat_hbm.at[t], lat_ref.at[t], lat_sem.at[t]) for t in range(t_n)]
    for copy in (*cot_copies, *lat_copies):
        copy.start()

    total = jnp.zeros((8, c_n), F32)
    for t in range(t_n):
        for r in range(r_n):
            slot = (t * r_n + r) % 2
            cot_copies[t * r_n + r].wait()
            wide[slot] = cot_ref[t, 2 * r].astype(F32) + cot_ref[t, 2 * r + 1].astype(F32)
            value = wide[slot, pl.ds(0, w_n, stride=2), :] + wide[slot, pl.ds(1, w_n, stride=2), :]
            total += jnp.sum(value.reshape(w_n // 8, 8, c_n), axis=0)
            grad_ref[t, r] = value.astype(BF16)
    bias_ref[...] = jnp.broadcast_to(jnp.sum(total, axis=0, keepdims=True), (8, c_n))

    total = jnp.zeros((8, c_n), F32)
    for t in range(t_n):
        lat_copies[t].wait()
        for r in range(r_n):
            total += jnp.sum(lat_ref[t, r].astype(F32).reshape(w_n // 8, 8, c_n), axis=0)
    mean = jnp.sum(total, axis=0, keepdims=True) / (t_n * r_n * w_n)
    square = jnp.zeros((8, c_n), F32)
    for t in range(t_n):
        for r in range(r_n):
            x = (lat_ref[t, r].astype(F32) - mean).reshape(w_n // 8, 8, c_n)
            square += jnp.sum(x * x, axis=0)
    square = jnp.sum(square, axis=0, keepdims=True)
    row = lax.broadcasted_iota(jnp.int32, (8, c_n), 0)
    stats = jnp.where(row == 0, mean, jnp.where(row == 1, square, 0.0))
    stats_ref[...] = stats
    for edge_ref, corner_ref, row in zip(edge_refs, corner_refs, facing_rows(edge_n, r_n)):
        corner_ref[...] = grad_ref[:, row]
        for t in range(t_n):
            edge_ref[pl.ds(t * w_n, w_n), :] = lat_ref[t, row]
            edge_ref[pl.ds((t_n + t) * w_n, w_n), :] = grad_ref[t, row]
        edge_ref[pl.ds(2 * t_n * w_n, TAB), :] = packed(stats)


def merged(a, b, cells):
    gap = a[0:1] - b[0:1]
    return (a[0:1] + b[0:1]) * 0.5, a[1:2] + b[1:2] + gap * gap * (cells / 4)


def merge_body(cells, a_ref, b_ref, out_ref):
    a = a_ref[...]
    if b_ref.shape[0] == 8:
        b = b_ref[...]
    else:
        a = unpacked(packed(a))
        b = unpacked(b_ref[b_ref.shape[0] - TAB :])
    mean, square = merged(a, b, cells)
    row = lax.broadcasted_iota(jnp.int32, a.shape, 0)
    out_ref[...] = jnp.where(row == 0, mean, jnp.where(row == 1, square, 0.0))


def lead_body(lat_ref, *rest):
    edge_refs, lead_ref = rest[:-1], rest[-1]
    t_n, r_n, w_n, _ = lat_ref.shape
    for t in range(t_n):
        for r in range(r_n):
            lead_ref[t, r] = lat_ref[t, r]
        for e, ref in enumerate(edge_refs):
            lead_ref[t, r_n + e] = ref[pl.ds(t * w_n, w_n), :]


def back_body(n_edge, n_h, grad_ref, halo_ref, kernel_ref, *rest):
    edge_refs, corner_refs, rest = rest[:n_edge], rest[n_edge : 2 * n_edge], rest[2 * n_edge :]
    fold, dact_ref, weight = rest
    t_n, r_n, w_n, c_n = grad_ref.shape
    h = lax.axis_index("height")
    top = (h == 0).astype(F32)
    bottom = (h == n_h - 1).astype(F32)
    first = (lax.axis_index("tm") == 0).astype(F32)

    def source(f, r):
        if 0 <= r < r_n:
            return (grad_ref[f, r] if f < t_n else halo_ref[f - t_n, r]).astype(F32)
        which = 0 if r < 0 else -1
        if f < t_n:
            value = edge_refs[which][pl.ds((t_n + f) * w_n, w_n), :]
        else:
            value = corner_refs[which][f - t_n]
        return value.astype(F32) * ((1.0 - top) if r < 0 else (1.0 - bottom))

    for j in range(3):
        for r in range(r_n):
            frame = []
            for f in range(t_n + 2):
                value = source(f, r + 1 - j)
                if j == 0 and r == 0:
                    value = value + source(f, 0) * top
                if j == 2 and r == r_n - 1:
                    value = value + source(f, r_n - 1) * bottom
                frame.append(value)
            for i in range(3):
                lanes = pl.ds((i * 3 + j) * c_n, c_n)
                for t in range(t_n):
                    value = frame[t + 2 - i]
                    if t == 0 and i < 2:
                        value = value + first * (frame[0] + frame[1] if i == 0 else frame[0])
                    fold[pl.ds((t * r_n + r) * w_n, w_n), lanes] = value.astype(BF16)

    for ij in range(9):
        weight[:, ij * c_n : (ij + 1) * c_n] = kernel_ref[ij // 3, ij % 3]
    for t in range(t_n):
        back = lax.dot_general(
            fold[pl.ds(t * r_n * w_n, r_n * w_n), :], weight[...], (((1,), (1,)), ((), ())),
            preferred_element_type=F32,
        )
        for r in range(r_n):
            slab = back[r * w_n : (r + 1) * w_n]
            low, mid, high = (slab[:, k * c_n : (k + 1) * c_n] for k in range(3))
            col = lax.broadcasted_iota(jnp.int32, low.shape, 0)
            dact_ref[t, r] = (
                mid + after(low, False) + before(high, False)
                + jnp.where(col == 0, low, 0.0) + jnp.where(col == w_n - 1, high, 0.0)
            )


def main_body(
    cells, n_h, n_t,
    lat_ref, fold_ref, dact_ref, gain_ref, shift_ref, bias_ref, *rest,
):
    stats_refs, rest = rest[:n_t], rest[n_t:]
    keep_ref, table_ref, dpre_ref, norm_ref = rest[:4]
    send_refs, (acts, sums) = rest[4 : 3 + n_h], rest[3 + n_h :]
    t_n, r_n, w_n, c_n = lat_ref.shape
    h = lax.axis_index("height")

    parts = [ref[...] for ref in stats_refs]
    of = cells // n_t
    while len(parts) > 1:
        of = of * 2
        parts = [
            jnp.concatenate(merged(parts[i], parts[i + 1], of), axis=0) for i in range(0, len(parts), 2)
        ]
    channel_mean, square = parts[0][0:1], parts[0][1:2]
    channel_mean = jnp.broadcast_to(channel_mean, (8, c_n))
    size = c_n // GROUPS
    mean = group_sum(channel_mean) * (1.0 / size)
    off = channel_mean - mean
    var = group_sum(jnp.broadcast_to(square, (8, c_n)) + off * off * cells) * (1.0 / (cells * size))
    rstd = lax.rsqrt(var + 1e-06)
    row = lax.broadcasted_iota(jnp.int32, (8, c_n), 0)
    norm_ref[...] = jnp.where(row == 0, mean, rstd)
    mean, rstd = mean[0:1], rstd[0:1]
    gain, shift = gain_ref[...], shift_ref[...]

    total_a = jnp.zeros((8, c_n), F32)
    total_b = jnp.zeros((8, c_n), F32)
    for t in range(t_n):
        for r in range(r_n):
            at = pl.ds((t * r_n + r) * w_n, w_n)
            hat = (lat_ref[t, r].astype(F32) - mean) * rstd
            pre = hat * gain + shift
            sig = jax.nn.sigmoid(pre)
            act = pre * sig
            acts[at, 0:c_n] = before(act, True).astype(BF16)
            acts[at, c_n : 2 * c_n] = act.astype(BF16)
            acts[at, 2 * c_n :] = after(act, True).astype(BF16)
            dpre = dact_ref[t, r] * sig * (1.0 + pre * (1.0 - sig))
            dpre_ref[t, r] = dpre
            total_a += jnp.sum((dpre * hat).reshape(w_n // 8, 8, c_n), axis=0)
            total_b += jnp.sum(dpre.reshape(w_n // 8, 8, c_n), axis=0)
    total_a = jnp.sum(total_a, axis=0, keepdims=True)
    total_b = jnp.sum(total_b, axis=0, keepdims=True)
    table = jnp.where(row == 0, bias_ref[...], jnp.where(row == 1, total_a, jnp.where(row == 2, total_b, 0.0)))
    table_ref[...] = table

    product = lax.dot_general(
        acts[...], fold_ref[...], (((0,), (0,)), ((), ())), preferred_element_type=F32
    )
    for ij in range(9):
        sums[pl.ds(ij * 3 * c_n, 3 * c_n), :] = product[:, ij * c_n : (ij + 1) * c_n]
    share = keep_ref.shape[0]
    if sums.shape[0] > 27 * c_n:
        sums[27 * c_n :, :] = jnp.zeros((sums.shape[0] - 27 * c_n, c_n), F32)
    keep_ref[...] = sums[pl.ds(h * share, share), :]
    for s, ref in enumerate(send_refs, 1):
        ref[0:share] = sums[pl.ds((h ^ s) * share, share), :].astype(BF16)
        ref[share:] = packed(table)


def first_sum_body(n_h, keep_ref, table_ref, *rest):
    got, (own_ref, out_table), sends = rest[: n_h - 1], rest[n_h - 1 : n_h + 1], rest[n_h + 1 : -1]
    total = rest[-1]
    share, piece = keep_ref.shape[0], own_ref.shape[0]
    value = keep_ref[...]
    for ref in got:
        value = value + ref[0:share].astype(F32)
    total[...] = value
    table = tree([unpacked(packed(table_ref[...]))] + [unpacked(ref[share:]) for ref in got])
    out_table[...] = table
    me = lax.axis_index("dp")
    own_ref[...] = total[pl.ds(me * piece, piece), :]
    for s, ref in enumerate(sends, 1):
        ref[0:piece] = total[pl.ds((me ^ s) * piece, piece), :].astype(BF16)
        ref[piece:] = packed(table)


def second_sum_body(own_ref, table_ref, token_ref, *rest):
    got, out_ref = rest[:-1], rest[-1]
    piece = own_ref.shape[0]
    value = own_ref[...]
    for ref in got:
        value = value + ref[0:piece].astype(F32)
    out_ref[0:piece] = value.astype(BF16)
    own = unpacked(packed(table_ref[...]))
    table = tree([own] + [unpacked(ref[piece:]) for ref in got])
    row = lax.broadcasted_iota(jnp.int32, table.shape, 0)
    kept = jnp.where(row == 0, table, jnp.where(row < 3, own, pltpu.roll(table, 2, 0)))
    out_ref[piece:] = packed(kept)


def pair_sum_body(a_ref, b_ref, out_ref):
    piece = a_ref.shape[0] - TAB
    out_ref[0:piece] = (a_ref[0:piece].astype(F32) + b_ref[0:piece].astype(F32)).astype(BF16)
    out_ref[piece:] = packed(unpacked(a_ref[piece:]) + unpacked(b_ref[piece:]))


def last_sum_body(a_ref, b_ref, out_ref, table_ref):
    piece = out_ref.shape[0]
    out_ref[...] = (a_ref[0:piece].astype(F32) + b_ref[0:piece].astype(F32)).astype(BF16)
    table_ref[...] = unpacked(a_ref[piece:]) + unpacked(b_ref[piece:])


def gather_body(token_ref, own_ref, *rest):
    got, out_ref = rest[:-1], rest[-1]
    piece = own_ref.shape[0]
    me = lax.axis_index("dp")
    for s, ref in enumerate((own_ref, *got)):
        out_ref[pl.ds((me ^ s) * piece, piece), :] = ref[...]


def spread_body(own_ref, *rest):
    got, out_ref = rest[:-1], rest[-1]
    share, rows = own_ref.shape[0], out_ref.shape[0]
    h = lax.axis_index("height")
    for s, ref in enumerate((own_ref, *got)):
        for q in range(1 + len(got)):

            def put(ref=ref, q=q):
                count = min(share, rows - q * share)
                out_ref[q * share : q * share + count] = ref[0:count].astype(F32)

            pl.when((h ^ s) == q)(put)


def place_body(mask, own_ref, *rest):
    out_hbm, wide, sem = rest[-3:]
    share = own_ref.shape[0]
    wide[...] = own_ref[...].astype(F32)
    at = (lax.axis_index("height") ^ mask) * share
    copy = pltpu.make_async_copy(wide, out_hbm.at[pl.ds(pl.multiple_of(at, 8), share)], sem)
    copy.start()
    copy.wait()


def forward_body(
    n_edge, n_h,
    lat_ref, past_ref, norm_ref, kernel_ref, gain_ref, shift_ref, offset_ref, after_ref, *rest,
):
    edge_refs, rest = rest[:n_edge], rest[n_edge:]
    out_ref, token_ref, acts, slabs, weight, wide = rest
    token_ref[...] = jnp.zeros_like(token_ref)
    t_n, r_n, w_n, c_n = lat_ref.shape
    h = lax.axis_index("height")
    mean, rstd = norm_ref[0:1], norm_ref[1:2]
    gain, shift = gain_ref[...], shift_ref[...]

    def silu(x):
        pre = (x.astype(F32) - mean) * rstd * gain + shift
        return (pre * jax.nn.sigmoid(pre)).astype(BF16)

    def act_of(f, r):
        if 0 <= r < r_n:
            return silu(past_ref[f, r] if f < 2 else lat_ref[f - 2, r])
        which = 0 if r < 0 else n_edge - 1
        if f < 2:
            return silu(past_ref[f, r_n + which])
        return silu(edge_refs[which][pl.ds((f - 2) * w_n, w_n), :])

    for f in range(t_n + 2):
        for r in range(-1, r_n + 1):
            acts[f, r + 1] = act_of(f, r)

    @pl.when(lax.axis_index("tm") == 0)
    def _():
        for f in range(2):
            for r in range(r_n + 2):
                acts[f, r] = acts[2, r]

    @pl.when(h == 0)
    def _():
        for f in range(t_n + 2):
            acts[f, 0] = acts[f, 1]

    @pl.when(h == n_h - 1)
    def _():
        for f in range(t_n + 2):
            acts[f, r_n + 1] = acts[f, r_n]

    for ij in range(9):
        i, j = ij // 3, ij % 3
        for k in range(3):
            weight[ij * c_n : (ij + 1) * c_n, k * c_n : (k + 1) * c_n] = kernel_ref[i, j, k * c_n : (k + 1) * c_n, :]
        for t in range(t_n):
            for r in range(r_n):
                slabs[(t * r_n + r) * w_n : (t * r_n + r + 1) * w_n, ij * c_n : (ij + 1) * c_n] = acts[t + i, r + j]
    offset = offset_ref[...]
    for t in range(t_n):
        value = jnp.dot(slabs[pl.ds(t * r_n * w_n, r_n * w_n), :], weight[...], preferred_element_type=F32)
        for r in range(r_n):
            slab = value[r * w_n : (r + 1) * w_n]
            low, mid, high = (slab[:, k * c_n : (k + 1) * c_n] for k in range(3))
            conv = before(low, True) + mid + after(high, True) + offset
            slot = r % 2
            conv = conv.astype(BF16).astype(F32)
            wide[slot, pl.ds(0, w_n, stride=2), :] = conv
            wide[slot, pl.ds(1, w_n, stride=2), :] = conv
            both = wide[slot].astype(BF16)
            out_ref[t, 2 * r] = both
            out_ref[t, 2 * r + 1] = both


def last_body(cells, dpre_ref, lat_ref, norm_ref, table_ref, gain_ref, out_ref, bias_ref, gains_ref, shifts_ref, token_ref):
    t_n, r_n, _, c_n = lat_ref.shape
    table, gain = table_ref[...], gain_ref[...]
    mean, rstd = norm_ref[0:1], norm_ref[1:2]
    scale = 1.0 / (cells * (c_n // GROUPS))
    means = group_sum(table * gain) * scale
    mean_b, mean_a = means[1:2], means[2:3]
    token_ref[...] = jnp.zeros_like(token_ref)
    bias_ref[...] = table[0:1]
    gains_ref[...] = table[3:4]
    shifts_ref[...] = table[4:5]
    for t in range(t_n):
        for r in range(r_n):
            hat = (lat_ref[t, r].astype(F32) - mean) * rstd
            out_ref[t, r] = (rstd * (dpre_ref[t, r] * gain - mean_a - hat * mean_b)).astype(BF16)


def local(latents, cotangent, group_norm_gain, group_norm_bias, kernel, kernel_bias):
    lat, cot = latents[0], cotangent[0]
    t_n, r_n, w_n, c_n = lat.shape
    n_dp, n_t, n_h = (lax.axis_size(axis) for axis in ("dp", "tm", "height"))
    n_edge = 1 if n_h == 2 else 2
    gain, shift, offset = (v.reshape(1, c_n) for v in (group_norm_gain, group_norm_bias, kernel_bias))
    grid = (t_n, r_n, w_n, c_n)
    edge = (t_n, w_n, c_n)
    small = shape((8, c_n), F32)
    rows = 27 * c_n
    unit = n_h * n_dp * 16
    total = -(-rows // unit) * unit
    share, piece = total // n_h, total // (n_h * n_dp)

    lat, grad, bias_part, stats, *edge_list = call(
        functools.partial(front_body, n_edge),
        [shape(grid, BF16), shape(grid, BF16), small, small]
        + [shape((2 * t_n * w_n + TAB, c_n), BF16)] * n_edge
        + [shape(edge, BF16)] * n_edge,
        pltpu.with_memory_space_constraint(cot, pltpu.HBM), pltpu.with_memory_space_constraint(lat, pltpu.HBM),
        scratch=[
            pltpu.VMEM(cot.shape, BF16),
            pltpu.VMEM((2, 2 * w_n, c_n), F32),
            pltpu.SemaphoreType.DMA((t_n * r_n,)),
            pltpu.SemaphoreType.DMA((t_n,)),
        ],
        far=(0, 1),
    )
    edge_list, corners = edge_list[:n_edge], edge_list[n_edge:]
    halo = moved(grad, 1, 0)
    edge_rows = facing(edge_list, 0)
    corner_rows = facing(corners, 1)

    cells = t_n * r_n * w_n
    for i in range(n_h.bit_length() - 1):
        other = edge_rows[0] if n_h == 2 else swap(stats, "height", 1 << i)
        cells = cells * 2
        (stats,) = call(functools.partial(merge_body, cells), [small], stats, other)
    cells = cells * n_t
    all_stats = [stats]
    for s in range(1, n_t):
        all_stats.append(swap(stats, "tm", s))
    (lead,) = call(lead_body, [shape((t_n, r_n + n_edge, w_n, c_n), BF16)], lat, *edge_rows)
    past = moved(lead, -1, 0)

    fold, dact = call(
        functools.partial(back_body, n_edge, n_h),
        [shape((t_n * r_n * w_n, 9 * c_n), BF16), shape(grid, F32)],
        grad, halo, kernel, *edge_rows, *corner_rows,
        scratch=[pltpu.VMEM((3 * c_n, 9 * c_n), BF16)],
        room=6 << 20,
        flops=2 * 27 * t_n * r_n * w_n * c_n * c_n,
    )
    keep, table, dpre, norm, *sends = call(
        functools.partial(main_body, cells, n_h, n_t),
        [shape((share, c_n), F32), small, shape(grid, F32), small]
        + [shape((share + TAB, c_n), BF16)] * (n_h - 1),
        lat, fold, dact, gain, shift, bias_part, *all_stats,
        scratch=[
            pltpu.VMEM((t_n * r_n * w_n, 3 * c_n), BF16),
            pltpu.VMEM((total, c_n), F32),
        ],
        room=8 << 20,
        flops=2 * 27 * t_n * r_n * w_n * c_n * c_n,
    )

    got = [swap(send, "height", s) for s, send in enumerate(sends, 1)]
    own, table, *sends = call(
        functools.partial(first_sum_body, n_h),
        [shape((piece, c_n), F32), small] + [shape((piece + TAB, c_n), BF16)] * (n_dp - 1),
        keep, table, *got,
        scratch=[pltpu.VMEM((share, c_n), F32)],
    )
    got = [swap(send, "dp", s) for s, send in enumerate(sends, 1)]
    upsampled, token = call(
        functools.partial(forward_body, n_edge, n_h),
        [shape(cot.shape, BF16), small],
        lat, past, norm, kernel, gain, shift, offset, table, *edge_rows,
        scratch=[
            pltpu.VMEM((t_n + 2, r_n + 2, w_n, c_n), BF16),
            pltpu.VMEM((t_n * r_n * w_n, 9 * c_n), BF16),
            pltpu.VMEM((9 * c_n, 3 * c_n), BF16),
            pltpu.VMEM((2, 2 * w_n, c_n), F32),
        ],
        room=6 << 20,
        flops=2 * 27 * t_n * r_n * w_n * c_n * c_n,
    )
    (part,) = call(second_sum_body, [shape((piece + TAB, c_n), BF16)], own, table, token, *got)
    distance = 1
    while distance < n_t:
        other = swap(part, "tm", distance)
        distance *= 2
        if distance < n_t:
            (part,) = call(pair_sum_body, [shape((piece + TAB, c_n), BF16)], part, other)
    part, table = call(last_sum_body, [shape((piece, c_n), BF16), small], part, other)
    got = [swap(part, "dp", s) for s in range(1, n_dp)]
    latent_gradient, bias_grad, gain_grad, shift_grad, token = call(
        functools.partial(last_body, cells),
        [shape(grid, BF16)] + [shape((1, c_n), F32)] * 3 + [small],
        dpre, lat, norm, table, gain,
    )
    (half,) = call(gather_body, [shape((share, c_n), BF16)], token, part, *got)
    got = [swap(half, "height", s) for s in range(1, n_h)]
    if n_h == 2 and total == rows:
        scratch = [pltpu.VMEM((share, c_n), F32), pltpu.SemaphoreType.DMA(())]
        (kernel_grad,) = call(
            functools.partial(place_body, 0), [shape((rows, c_n), F32)], half, scratch=scratch, far_out=(0,)
        )
        (kernel_grad,) = call(
            functools.partial(place_body, 1), [shape((rows, c_n), F32)], *got, kernel_grad,
            scratch=scratch, far=(1,), far_out=(0,), alias={1: 0},
        )
    else:
        (kernel_grad,) = call(spread_body, [shape((rows, c_n), F32)], half, *got)
    return (
        upsampled[None],
        latent_gradient[None],
        kernel_grad.reshape(kernel.shape),
        bias_grad.reshape(c_n),
        gain_grad.reshape(c_n),
        shift_grad.reshape(c_n),
    )


def solution(mesh):
    split = P("dp", "tm", "height", None, None)
    return jax.shard_map(
        local,
        mesh=mesh,
        in_specs=(split, split, P(), P(), P(), P()),
        out_specs=(split, split, P(), P(), P(), P()),
        check_vma=False,
    )
```
